32 devices in a mesh: narrow: 4 (over y, x), wide: 8 (over z, core).
Axes of the slice: x: 2, y: 2, z: 4, core: 2. Of those that a mesh axis runs over, the one named last changes fastest.
Arguments:
- tokens: bfloat16 [16, 1024, 1024], P('narrow', 'wide'), may hold values from -6 to 6
- resets: int32 [16, 1024], P('narrow', 'wide'), may hold values 0 or 1
- norm1_gain: float32 [1024], replicated, may hold values from 0.5 to 1.5
- ema_delta: float32 [1024, 16], replicated, may hold values from -6 to 0.2, as said below
- ema_alpha: float32 [1024, 16], replicated, may hold values from -6 to 0.2, as said below
- ema_beta: float32 [1024, 16], replicated, may hold values from -5 to 5
- ema_eta: float32 [1024, 16], replicated, may hold values from -5 to 5
- ema_omega: float32 [1024], replicated, may hold values from -5 to 5
- w_value: bfloat16 [1024, 2048], replicated, may hold values from -0.1875 to 0.1875
- w_mix: bfloat16 [1024, 4224], replicated, may hold values from -0.1875 to 0.1875
- qk_affine: float32 [128, 3], replicated, may hold values from -8 to 8
- w_hidden: bfloat16 [2048, 1024], replicated, may hold values from -0.5 to 0.5
- norm2_gain: float32 [1024], replicated, may hold values from 0.5 to 1.5
- w_ffn_in: bfloat16 [1024, 4096], replicated, may hold values from -0.1875 to 0.1875
- w_ffn_out: bfloat16 [4096, 1024], replicated, may hold values from -0.09375 to 0.09375
- cotangent: bfloat16 [16, 1024, 1024], P('narrow', 'wide'), may hold values from -6 to 6
Outputs:
- layer_output: bfloat16 [16, 1024, 1024], P('narrow', 'wide')
- tokens_grad: float32 [16, 1024, 1024], P('narrow', 'wide')
- grad_norm1_gain: float32 [1024], P('wide')
- grad_ema_delta: float32 [1024, 16], P('wide')
- grad_ema_alpha: float32 [1024, 16], P('wide')
- grad_ema_beta: float32 [1024, 16], P('wide')
- grad_ema_eta: float32 [1024, 16], P('wide')
- grad_ema_omega: float32 [1024], P('wide')
- grad_w_value: float32 [1024, 2048], P('wide')
- grad_w_mix: float32 [1024, 4224], P('wide')
- grad_qk_affine: float32 [128, 3], P('wide')
- grad_w_hidden: float32 [2048, 1024], P('wide')
- grad_norm2_gain: float32 [1024], P('wide')
- grad_w_ffn_in: float32 [1024, 4096], P('wide')
- grad_w_ffn_out: float32 [4096, 1024], P('wide')
The draws below stay inside these ranges and needn't reach their ends.
Inputs may be any that keep to these rules, and one draw needn't show every extreme that they name: `ema_delta`: raw decay parameter. `ema_alpha`: raw decay parameter.
All inputs are finite; a program needn't handle non-finite values. No bound on the sum of `resets` on one device may be relied on, other than what follows from the above.
Results may differ from the reference program's by a relative error of at most 0.015.
The reference program's roundings to bfloat16 on the way count: a program that leaves them out, or rounds other values in their place, can miss the bound.
Values sent between devices are 32-bit elements; how exact they have to be, the bound alone decides.
No kernel may reach another device: no remote copies, remote signals or barrier semaphores. Data moves between devices by JAX's collectives and lax.ppermute only.
A program may use at most 256 MiB of HBM per device.

```python
import math
import jax
import jax.numpy as jnp
from jax import lax

D = 1024
Z = 128
VALUE_WIDTH = 2048
H = 16
FF = 4096
BLOCK_TOKENS = 128
LENGTH = 1024
SEGS = 16


def decay_pair(key):
    folded = jax.random.fold_in(key, 11)
    pick_key, rate_key, tilt_key = jax.random.split(folded, 3)
    slow_share = 0.5
    slower = jax.random.uniform(pick_key, (D, 1)) < slow_share
    spread = jax.random.uniform(rate_key, (D, H))
    slow_log = jnp.log(0.3 / LENGTH) + spread * jnp.log(2.0 / 0.3)
    fast_log = jnp.log(1.0 / 50.0) + spread * jnp.log(5.0)
    log_rate = jnp.where(slower, slow_log, fast_log)
    tilted = jax.random.uniform(tilt_key, (D, H), minval=-0.5, maxval=0.5)
    retain = jnp.exp(0.5 * log_rate + tilted)
    damping = jnp.exp(0.5 * log_rate - tilted)
    return (jnp.log(retain / (1.0 - retain)), jnp.log(damping / (1.0 - damping)))


def draw_ema_delta(key, part):
    return decay_pair(key)[0]


def draw_ema_alpha(key, part):
    return decay_pair(key)[1]


def place_ends(array, rng, smallest, top_value):
    extent = array.shape
    place = [jax.random.randint(jax.random.fold_in(rng, axis), (), 0, extent[axis]) for axis in range(len(extent))]
    array = array.at[tuple(place)].set(smallest)
    longest = extent.index(max(extent))
    place[longest] = (place[longest] + 1) % extent[longest]
    return array.at[tuple(place)].set(top_value)


def block_levels(stream_key, extent, cuts, smallest, largest):
    def one(dim, parts):
        heights = jax.random.uniform(jax.random.fold_in(jax.random.fold_in(stream_key, 6), dim), (parts,), jnp.float32, smallest / len(cuts), largest / len(cuts))
        return jnp.repeat(jnp.exp(heights), extent[dim] // parts).reshape((-1,) + (1,) * (len(extent) - dim - 1))

    level = one(*cuts[0])
    for cut in cuts[1:]:
        level = level * one(*cut)
    return level


def gaussian(rng, dims, width, most, cuts=(), kind=jnp.bfloat16):
    values = width * jax.random.normal(rng, dims, jnp.float32)
    if cuts:
        values = values * block_levels(rng, dims, cuts, -0.22, 0.18)
    return jnp.clip(values, -most, most).astype(kind)


def setup_inputs(seed: int = 0) -> dict:
    key_list = jax.random.split(jax.random.key(seed), 17)
    return {
        "tokens": gaussian(key_list[0], (SEGS, LENGTH, D), 1.0, 6.0, ((0, 4), (1, 8))),
        "resets": place_ends((jax.random.randint(key_list[1], (SEGS, LENGTH), 0, 4 * BLOCK_TOKENS) < 1).astype(jnp.int32), jax.random.fold_in(key_list[1], 1), 0, 1),
        "norm1_gain": jnp.clip(1.0 + 0.1 * jax.random.normal(key_list[2], (D,), jnp.float32), 0.5, 1.5),
        "ema_delta": draw_ema_delta(jax.random.fold_in(key_list[16], 71), 0),
        "ema_alpha": draw_ema_alpha(jax.random.fold_in(key_list[16], 71), 0),
        "ema_beta": gaussian(key_list[5], (D, H), 1.0, 5.0, (), jnp.float32),
        "ema_eta": gaussian(key_list[6], (D, H), 1.0, 5.0, (), jnp.float32),
        "ema_omega": gaussian(key_list[7], (D,), 1.0, 5.0, (), jnp.float32),
        "w_value": gaussian(key_list[8], (D, VALUE_WIDTH), D ** -0.5, 0.1875),
        "w_mix": gaussian(key_list[9], (D, 2 * D + Z + VALUE_WIDTH), D ** -0.5, 0.1875),
        "qk_affine": gaussian(key_list[10], (Z, 3), 2.0, 8.0, (), jnp.float32),
        "w_hidden": gaussian(key_list[11], (VALUE_WIDTH, D), (VALUE_WIDTH // 16) ** -0.5, 0.5),
        "norm2_gain": jnp.clip(1.0 + 0.1 * jax.random.normal(key_list[12], (D,), jnp.float32), 0.5, 1.5),
        "w_ffn_in": gaussian(key_list[13], (D, FF), D ** -0.5, 0.1875),
        "w_ffn_out": gaussian(key_list[14], (FF, D), FF ** -0.5, 0.09375),
        "cotangent": gaussian(key_list[15], (SEGS, LENGTH, D), 1.0, 6.0, ((0, 4), (1, 8))),
    }


@jax.custom_vjp
def low(v):
    return lax.optimization_barrier(v.astype(jnp.bfloat16)).astype(jnp.float32)

@jax.custom_vjp
def narrow_backward(v):
    return v

def low_keep(v):
    return (low(v), None)

def low_pass(kept, grad):
    return (grad,)

def back_keep(v):
    return (v, None)

def back_low(kept, grad):
    return (low(grad),)
low.defvjp(low_keep, low_pass)
narrow_backward.defvjp(back_keep, back_low)
EPSILON = 1e-05
FLOOR = -1e+30
EXACT_PRECISION = lax.Precision.HIGHEST

def highest_dot(left, right):
    return jnp.dot(left, right, precision=EXACT_PRECISION, preferred_element_type=jnp.float32)

def layer_norm(value_rows, norm_gain):
    row_mean = lax.optimization_barrier(jnp.mean(value_rows, axis=-1, keepdims=True))
    centred = value_rows - row_mean
    variance = lax.optimization_barrier(jnp.mean(centred * centred, axis=-1, keepdims=True))
    return centred * lax.rsqrt(variance + EPSILON) * norm_gain

def ema_block(inputs, resets, carried, ema_delta, ema_alpha, ema_beta, ema_eta):
    step_count = inputs.shape[0]
    retain = jax.nn.sigmoid(ema_delta)
    damping = jax.nn.sigmoid(ema_alpha)
    log_decay = jnp.log1p(-retain * damping)
    counts = jnp.cumsum(resets)
    position = jnp.arange(step_count, dtype=jnp.int32)
    allowed = ((position[:, None] >= position[None, :]) & (counts[:, None] == counts[None, :])).astype(jnp.float32)
    offsets = (position - step_count // 2).astype(jnp.float32)
    growing = jnp.exp(offsets[:, None, None] * log_decay)
    shrinking = jnp.exp(-offsets[:, None, None] * log_decay)
    weighted = (retain * ema_beta)[None] * shrinking * inputs[:, :, None]
    summed = highest_dot(allowed, weighted.reshape(step_count, -1)).reshape(weighted.shape)
    leading = (counts == 0).astype(jnp.float32)
    powers = jnp.exp((position + 1).astype(jnp.float32)[:, None, None] * log_decay)
    states = growing * summed + leading[:, None, None] * powers * carried[None]
    output = lax.optimization_barrier(jnp.sum(states * ema_eta[None], axis=2)) * (1.0 / math.sqrt(ema_eta.shape[1]))
    return (output, states[-1])

def mega_layer(inputs, resets, params):
    norm1_gain, ema_delta, ema_alpha, ema_beta, ema_eta, ema_omega, w_value, w_mix, qk_affine, w_hidden, norm2_gain, w_ffn_in, w_ffn_out = params
    normed = layer_norm(inputs, norm1_gain)
    value_pre = narrow_backward(highest_dot(low(normed), w_value))
    value_rows = low(jax.nn.silu(value_pre))
    normed_blocks = normed.reshape(-1, BLOCK_TOKENS, D)
    reset_blocks = resets.reshape(-1, BLOCK_TOKENS)

    def ema_step(carried, pieces):
        output, end_state = ema_block(pieces[0], pieces[1], carried, ema_delta, ema_alpha, ema_beta, ema_eta)
        return (end_state, output)
    unused, smoothed = lax.scan(jax.checkpoint(ema_step), jnp.zeros((D, H), jnp.float32), (normed_blocks, reset_blocks))
    smoothed = smoothed.reshape(-1, D)
    mixed_pre = smoothed + ema_omega * normed
    mixed = low(jax.nn.silu(mixed_pre))
    mixed_proj = narrow_backward(highest_dot(mixed, w_mix))
    update = jax.nn.sigmoid(mixed_proj[:, :D])
    shared = jax.nn.silu(mixed_proj[:, D:D + Z + VALUE_WIDTH])
    latent = shared[:, :Z]
    reset_gate = shared[:, Z:]
    hidden_part = mixed_proj[:, D + Z + VALUE_WIDTH:]
    score_scale = 1.0 / math.sqrt(Z)
    query_rows = low((latent * qk_affine[:, 0] + qk_affine[:, 2]) * score_scale).reshape(-1, BLOCK_TOKENS, Z)
    key_matrix = low(latent * qk_affine[:, 1]).reshape(-1, BLOCK_TOKENS, Z)
    counts = jnp.cumsum(reset_blocks, axis=1)
    position = jnp.arange(BLOCK_TOKENS, dtype=jnp.int32)
    allowed = (position[:, None] >= position[None, :])[None] & (counts[:, :, None] == counts[:, None, :])
    attention_scores = narrow_backward(jnp.einsum('agd,ald->agl', query_rows, key_matrix, precision=EXACT_PRECISION))
    attention_scores = jnp.where(allowed, attention_scores, FLOOR)
    row_top = lax.optimization_barrier(jnp.max(attention_scores, axis=-1, keepdims=True))
    exponent = jnp.exp(attention_scores - row_top)
    attention_probabilities = low(exponent / lax.optimization_barrier(jnp.sum(exponent, axis=-1, keepdims=True)))
    attention_output = narrow_backward(jnp.einsum('ycl,ylu->ycu', attention_probabilities, value_rows.reshape(-1, BLOCK_TOKENS, VALUE_WIDTH), precision=EXACT_PRECISION)).reshape(-1, VALUE_WIDTH)
    gated = low(attention_output * reset_gate)
    hidden_add = narrow_backward(highest_dot(gated, w_hidden))
    hidden = jax.nn.silu(hidden_part + hidden_add)
    first_out = inputs + update * (hidden - inputs)
    normed_two = low(layer_norm(first_out, norm2_gain))
    ffn_pre = narrow_backward(highest_dot(normed_two, w_ffn_in))
    ffn_act = low(jax.nn.silu(ffn_pre))
    ffn_out = narrow_backward(highest_dot(ffn_act, w_ffn_out))
    return first_out + ffn_out

def reference(tokens, resets, norm1_gain, ema_delta, ema_alpha, ema_beta, ema_eta, ema_omega, w_value, w_mix, qk_affine, w_hidden, norm2_gain, w_ffn_in, w_ffn_out, cotangent):
    weights = tuple((weight.astype(jnp.float32) for weight in (norm1_gain, ema_delta, ema_alpha, ema_beta, ema_eta, ema_omega, w_value, w_mix, qk_affine, w_hidden, norm2_gain, w_ffn_in, w_ffn_out)))

    def per_segment(totals, pieces):
        seg_tokens, seg_resets, seg_grad = pieces

        def forward(inputs, *params):
            return mega_layer(inputs, seg_resets, params)
        outputs, pullback = jax.vjp(forward, seg_tokens.astype(jnp.float32), *weights)
        gradients = pullback(seg_grad.astype(jnp.float32))
        new_totals = tuple((earlier_sum + added for earlier_sum, added in zip(totals, gradients[1:])))
        return (new_totals, (outputs.astype(jnp.bfloat16), gradients[0]))
    zeros = tuple((jnp.zeros_like(weight) for weight in weights))
    totals, stacked = lax.scan(per_segment, zeros, (tokens, resets, cotangent))
    return (stacked[0], stacked[1], totals[0], totals[1], totals[2], totals[3], totals[4], totals[5], totals[6], totals[7], totals[8], totals[9], totals[10], totals[11], totals[12])
```

```python
import math

import jax
import jax.numpy as jnp
from jax import lax
from jax.experimental import pallas as pl
from jax.experimental.pallas import tpu as pltpu
from jax.sharding import PartitionSpec as P

EPSILON = 1e-05
FLOOR = -1e30


def product(left, right):
    return jnp.dot(left, right, preferred_element_type=jnp.float32)


def contract_rows(left, right):
    return lax.dot_general(
        left, right, (((0,), (0,)), ((), ())), preferred_element_type=jnp.float32
    )


def times_transpose(left, right):
    return lax.dot_general(
        left, right, (((1,), (1,)), ((), ())), preferred_element_type=jnp.float32
    )


def silu_slope(value_rows):
    logistic = jax.nn.sigmoid(value_rows)
    return logistic * (1.0 + value_rows * (1.0 - logistic))


def layer_norm(value_rows, norm_gain):
    row_mean = jnp.mean(value_rows, axis=-1, keepdims=True)
    centred = value_rows - row_mean
    variance = jnp.mean(centred * centred, axis=-1, keepdims=True)
    inverse = lax.rsqrt(variance + EPSILON)
    standard = centred * inverse
    return (standard * norm_gain, standard, inverse)


def norm_back(grad_out, standard, inverse, norm_gain):
    scaled = grad_out * norm_gain
    first_mean = jnp.mean(scaled, axis=-1, keepdims=True)
    second_mean = jnp.mean(scaled * standard, axis=-1, keepdims=True)
    return (
        inverse * (scaled - first_mean - standard * second_mean),
        jnp.sum(grad_out * standard, axis=0),
    )


SCALARS = pl.BlockSpec(memory_space=pltpu.SMEM)


def scan_ends(rows, live, decay, reverse):
    segs, steps = rows.shape[:2]
    tile = rows.shape[2:]
    dims = decay.shape[0]

    def kernel(live_ref, rows_ref, decay_ref, out_ref):
        seg = pl.program_id(0)
        decay_now = decay_ref[...]

        def step(i, state):
            t = steps - 1 - i if reverse else i
            return decay_now * state + (live_ref[seg, t] * rows_ref[0, t])[None]

        state = lax.fori_loop(0, steps, step, jnp.zeros_like(decay_now), unroll=8)
        out_ref[0] = decay_now * state if reverse else state

    return pl.pallas_call(
        kernel,
        grid=(segs,),
        in_specs=[
            SCALARS,
            pl.BlockSpec((1, steps) + tile, lambda s: (s, 0, 0, 0)),
            pl.BlockSpec((dims,) + tile, lambda s: (0, 0, 0)),
        ],
        out_specs=pl.BlockSpec((1, dims) + tile, lambda s: (s, 0, 0, 0)),
        out_shape=jax.ShapeDtypeStruct((segs, dims) + tile, jnp.float32),
        name="ema_ends",
    )(live, rows, decay)


def scan_sum(rows, keep_next, decay, weight, entry, reverse):
    segs, steps = rows.shape[:2]
    tile = rows.shape[2:]
    dims = decay.shape[0]

    def kernel(keep_ref, rows_ref, decay_ref, weight_ref, entry_ref, out_ref):
        seg = pl.program_id(0)
        decay_now = decay_ref[...]
        weight_now = weight_ref[...]

        def step(i, carry):
            t = steps - 1 - i if reverse else i
            state = carry + rows_ref[0, t][None]
            out_ref[0, t] = jnp.sum(weight_now * state, axis=0)
            return (decay_now * state) * keep_ref[seg, t]

        lax.fori_loop(0, steps, step, entry_ref[0], unroll=4)

    by_seg = pl.BlockSpec((1, steps) + tile, lambda s: (s, 0, 0, 0))
    by_dim = pl.BlockSpec((dims,) + tile, lambda s: (0, 0, 0))
    return pl.pallas_call(
        kernel,
        grid=(segs,),
        in_specs=[
            SCALARS,
            by_seg,
            by_dim,
            by_dim,
            pl.BlockSpec((1, dims) + tile, lambda s: (s, 0, 0, 0)),
        ],
        out_specs=by_seg,
        out_shape=jax.ShapeDtypeStruct(rows.shape, jnp.float32),
        name="ema_scan",
    )(keep_next, rows, decay, weight, entry)


def scan_grads(rows, grads, keep_next, decay, entry, later):
    segs, steps = rows.shape[:2]
    tile = rows.shape[2:]
    dims = decay.shape[0]
    half = dims // 2

    def kernel(keep_ref, rows_ref, grad_ref, decay_ref, entry_ref, later_ref, g_ref, m_ref):
        seg = pl.program_id(1)
        decay_now = decay_ref[...]

        @pl.when(seg == 0)
        def _():
            g_ref[...] = jnp.zeros_like(g_ref)
            m_ref[...] = jnp.zeros_like(m_ref)

        entry_now = entry_ref[0]

        def step(t, carry):
            from_before, tangent, g_sum, m_sum = carry
            grad = grad_ref[0, t][None]
            keep = keep_ref[seg, t]
            state = from_before + rows_ref[0, t][None]
            g_sum = g_sum + state * grad
            m_sum = m_sum + tangent * grad
            return (
                (decay_now * state) * keep,
                (state + decay_now * tangent) * keep,
                g_sum,
                m_sum,
            )

        from_before, tangent, g_sum, m_sum = lax.fori_loop(
            0,
            steps - 1,
            step,
            (decay_now * entry_now, entry_now, g_ref[...], m_ref[...]),
            unroll=4,
        )
        grad = grad_ref[0, steps - 1][None]
        state = from_before + rows_ref[0, steps - 1][None]
        g_ref[...] = g_sum + state * grad
        m_ref[...] = m_sum + tangent * grad + later_ref[0] * tangent

    by_seg = pl.BlockSpec((1, steps) + tile, lambda j, s: (s, 0, 0, 0))
    by_dim = pl.BlockSpec((half,) + tile, lambda j, s: (j, 0, 0))
    both = pl.BlockSpec((1, half) + tile, lambda j, s: (s, j, 0, 0))
    return pl.pallas_call(
        kernel,
        grid=(2, segs),
        in_specs=[SCALARS, by_seg, by_seg, by_dim, both, both],
        out_specs=[by_dim, by_dim],
        out_shape=[jax.ShapeDtypeStruct((dims,) + tile, jnp.float32)] * 2,
        name="ema_grads",
    )(keep_next, rows, grads, decay, entry, later)


def entering(ends, whole_keep, block_decay, axis, reverse):
    count = lax.axis_size(axis)
    place = lax.axis_index(axis)
    flags = jnp.broadcast_to(whole_keep[:, None, None, None], ends[:, :1].shape)
    gathered = lax.all_gather(jnp.concatenate([ends, flags], axis=1), axis)
    state = jnp.zeros_like(ends)
    order = range(count - 1, -1, -1) if reverse else range(count)
    for k in order:
        joined = gathered[k, :, :-1] + block_decay[None] * gathered[k, :, -1:] * state
        state = jnp.where(k > place if reverse else k < place, joined, state)
    return state


def weight_grad(left, right, chips, side, quarter, columns, added):
    tokens, rows = left.shape
    block_rows = rows // (2 * chips)
    tile_n = 512 if block_rows <= 128 else 256
    tile_n = min(tile_n, columns)
    per_quarter = columns // tile_n

    def kernel(picks_ref, *refs):
        left_refs = refs[:chips]
        right_ref = refs[chips]
        add_refs = refs[chips + 1 : -1]
        out_ref = refs[-1]
        whole_left = jnp.concatenate([ref[...] for ref in left_refs], axis=1)
        total = lax.dot_general(
            whole_left,
            right_ref[...],
            (((0,), (0,)), ((), ())),
            preferred_element_type=jnp.float32,
        ).reshape(out_ref.shape)
        for ref in add_refs:
            total = total + ref[...]
        out_ref[...] = total

    def left_spec(chip):
        return pl.BlockSpec((tokens, block_rows), lambda j, picks: (0, 2 * chip + picks[0]))

    def wide_spec(shape):
        return pl.BlockSpec(shape, lambda j, picks: (0, 0, picks[1] * per_quarter + j))

    add_specs = []
    for part in added:
        if part.shape[2] == columns:
            add_specs.append(
                pl.BlockSpec((chips, block_rows, tile_n), lambda j, picks: (0, 0, j))
            )
        else:
            add_specs.append(wide_spec((chips, block_rows, tile_n)))
    return pl.pallas_call(
        kernel,
        grid_spec=pltpu.PrefetchScalarGridSpec(
            num_scalar_prefetch=1,
            grid=(per_quarter,),
            in_specs=[left_spec(chip) for chip in range(chips)]
            + [
                pl.BlockSpec(
                    (tokens, tile_n), lambda j, picks: (0, picks[1] * per_quarter + j)
                )
            ]
            + add_specs,
            out_specs=pl.BlockSpec((chips, block_rows, tile_n), lambda j, picks: (0, 0, j)),
        ),
        out_shape=jax.ShapeDtypeStruct((chips, block_rows, columns), jnp.float32),
        name="weight_grad",
    )(jnp.stack([side, quarter]).astype(jnp.int32), *([left] * chips), right, *added)


def ring_scatter(part, place, chips, towards):
    perm = [
        (2 * chip + core, 2 * ((chip + towards) % chips) + core)
        for chip in range(chips)
        for core in range(2)
    ]

    def pick(k):
        return lax.dynamic_index_in_dim(part, (place + k * chips - towards * k) % chips, 0, False)

    total = pick(1)
    for k in range(2, chips + 1):
        total = lax.ppermute(total, "wide", perm) + pick(k)
    return total


def reduced_quarters(left, right):
    wide = lax.axis_size("wide")
    chips = wide // 2
    columns = right.shape[1]
    place = lax.axis_index("wide") // 2
    core = lax.axis_index("wide") % 2
    first = lax.axis_index("narrow") % 2
    second = lax.axis_index("narrow") // 2
    cores = [(i, i ^ 1) for i in range(wide)]
    swaps = [[(i, i ^ 1) for i in range(4)], [(i, i ^ 2) for i in range(4)]]
    zero = jnp.zeros_like(core)
    quarter = columns // 4
    sent = weight_grad(left, right, chips, 1 - core, zero, columns, [])
    from_core = lax.ppermute(sent, "wide", cores)
    quarters = []
    for half, place_in in ((0, first), (1, second)):
        away = weight_grad(
            left, right, chips, core, 2 * half + 1 - place_in, quarter, [from_core]
        )
        got = lax.ppermute(away, "narrow", swaps[half])
        mine = weight_grad(
            left, right, chips, core, 2 * half + place_in, quarter, [from_core, got]
        )
        total = ring_scatter(mine, place, chips, 1 if half == 0 else -1)
        total = total + lax.ppermute(total, "narrow", swaps[1 - half])
        other = lax.ppermute(total, "narrow", swaps[half])
        quarters += [
            jnp.where(place_in == 0, total, other),
            jnp.where(place_in == 0, other, total),
        ]
    return quarters


def reduced_plain(left, right):
    share = lax.psum_scatter(
        contract_rows(left, right), "wide", scatter_dimension=0, tiled=True
    )
    total = lax.psum(share, "narrow")
    quarter = right.shape[1] // 4
    return [total[:, k * quarter : (k + 1) * quarter] for k in range(4)]


def reduced_small(parts):
    packed = jnp.concatenate(parts, axis=1)
    share = lax.psum_scatter(packed, "wide", scatter_dimension=0, tiled=True)
    total = lax.psum(share, "narrow")[0]
    outs = []
    at = 0
    for part in parts:
        outs.append(total[at : at + part.shape[1]])
        at += part.shape[1]
    return outs


def per_device(
    tokens,
    resets,
    norm1_gain,
    ema_delta,
    ema_alpha,
    ema_beta,
    ema_eta,
    ema_omega,
    w_value,
    w_mix,
    qk_affine,
    w_hidden,
    norm2_gain,
    w_ffn_in,
    w_ffn_out,
    cotangent,
):
    tuned = lax.axis_size("narrow") == 4 and lax.axis_size("wide") == 8
    wide = lax.axis_size("wide")
    seg_count, step_count, model_width = tokens.shape
    latent_width = qk_affine.shape[0]
    value_width = w_value.shape[1]
    row_count = seg_count * step_count
    reduce_big = reduced_quarters if tuned else reduced_plain
    inputs = tokens.reshape(row_count, model_width).astype(jnp.float32)
    normed, standard_one, inverse_one = layer_norm(inputs, norm1_gain)
    normed_low = normed.astype(jnp.bfloat16)
    value_pre = product(normed_low, w_value)
    values_low = jax.nn.silu(value_pre).astype(jnp.bfloat16)
    dims = ema_delta.shape[1]
    tile = (model_width // 128, 128)
    retain = jax.nn.sigmoid(ema_delta)
    damping = jax.nn.sigmoid(ema_alpha)
    decay = (1.0 - retain * damping).T.reshape((dims,) + tile)
    block_decay = jnp.exp(step_count * jnp.log1p(-retain * damping)).T.reshape((dims,) + tile)
    weight = (ema_eta * retain * ema_beta * (1.0 / math.sqrt(dims))).T.reshape((dims,) + tile)
    counts = jnp.cumsum(resets, axis=1)
    keep = 1.0 - resets.astype(jnp.float32)
    keep_next = jnp.concatenate([keep[:, 1:], jnp.ones_like(keep[:, :1])], axis=1)
    last_run = (counts == counts[:, -1:]).astype(jnp.float32)
    first_run = (counts == 0).astype(jnp.float32)
    whole_keep = first_run[:, -1]
    normed_tiles = normed.reshape((seg_count, step_count) + tile)
    ends = scan_ends(normed_tiles, last_run, decay, False)
    entry = keep[:, :1, None, None] * entering(ends, whole_keep, block_decay, "wide", False)
    smoothed = scan_sum(
        normed_tiles, keep_next, decay, weight, decay[None] * entry, False
    ).reshape(row_count, model_width)
    mixed_pre = smoothed + ema_omega * normed
    mixed_low = jax.nn.silu(mixed_pre).astype(jnp.bfloat16)
    mixed_proj = product(mixed_low, w_mix)
    split_two = model_width + latent_width + value_width
    update = jax.nn.sigmoid(mixed_proj[:, :model_width])
    shared_pre = mixed_proj[:, model_width:split_two]
    shared = jax.nn.silu(shared_pre)
    latent = shared[:, :latent_width]
    reset_gate = shared[:, latent_width:]
    hidden_part = mixed_proj[:, split_two:]
    score_scale = 1.0 / math.sqrt(latent_width)
    query_rows = (
        ((latent * qk_affine[:, 0] + qk_affine[:, 2]) * score_scale)
        .astype(jnp.bfloat16)
        .reshape(seg_count, step_count, latent_width)
    )
    key_matrix = (
        (latent * qk_affine[:, 1]).astype(jnp.bfloat16).reshape(seg_count, step_count, latent_width)
    )
    position = jnp.arange(step_count, dtype=jnp.int32)
    allowed = (position[:, None] >= position[None, :])[None] & (
        counts[:, :, None] == counts[:, None, :]
    )
    attention_scores = jnp.einsum(
        "sqz,skz->sqk", query_rows, key_matrix, preferred_element_type=jnp.float32
    )
    attention_scores = jnp.where(allowed, attention_scores, FLOOR)
    row_top = jnp.max(attention_scores, axis=-1, keepdims=True)
    exponent = jnp.exp(attention_scores - row_top)
    attention_probabilities = exponent / jnp.sum(exponent, axis=-1, keepdims=True)
    probabilities_narrow = attention_probabilities.astype(jnp.bfloat16)
    value_sequence = values_low.reshape(seg_count, step_count, value_width)
    attention_output = jnp.einsum(
        "jmo,joe->jme", probabilities_narrow, value_sequence, preferred_element_type=jnp.float32
    ).reshape(row_count, value_width)
    gated_low = (attention_output * reset_gate).astype(jnp.bfloat16)
    hidden_pre = hidden_part + product(gated_low, w_hidden)
    hidden = jax.nn.silu(hidden_pre)
    first_out = inputs + update * (hidden - inputs)
    normed_two, standard_two, inverse_two = layer_norm(first_out, norm2_gain)
    normed_two_low = normed_two.astype(jnp.bfloat16)
    ffn_pre = product(normed_two_low, w_ffn_in)
    ffn_low = jax.nn.silu(ffn_pre).astype(jnp.bfloat16)
    result = (
        (first_out + product(ffn_low, w_ffn_out))
        .astype(jnp.bfloat16)
        .reshape(seg_count, step_count, model_width)
    )
    out_grad_low = cotangent.reshape(row_count, model_width)
    out_grad = out_grad_low.astype(jnp.float32)
    grad_ffn_out_w = reduce_big(ffn_low, out_grad_low)
    grad_ffn_pre_low = (times_transpose(out_grad_low, w_ffn_out) * silu_slope(ffn_pre)).astype(
        jnp.bfloat16
    )
    grad_ffn_in_w = reduce_big(normed_two_low, grad_ffn_pre_low)
    grad_normed_two = times_transpose(grad_ffn_pre_low, w_ffn_in)
    grad_first_norm, grad_norm2 = norm_back(grad_normed_two, standard_two, inverse_two, norm2_gain)
    grad_first = out_grad + grad_first_norm
    grad_residual = grad_first * (1.0 - update)
    grad_update = grad_first * (hidden - inputs)
    grad_hidden_pre = grad_first * update * silu_slope(hidden_pre)
    grad_add_low = grad_hidden_pre.astype(jnp.bfloat16)
    grad_hidden_w = reduce_big(gated_low, grad_add_low)
    grad_gated = times_transpose(grad_add_low, w_hidden)
    gradient_attention_narrow = (
        (grad_gated * reset_gate).astype(jnp.bfloat16).reshape(seg_count, step_count, value_width)
    )
    grad_gate = grad_gated * attention_output
    grad_probs = jnp.einsum(
        "fjb,fyb->fjy",
        gradient_attention_narrow,
        value_sequence,
        preferred_element_type=jnp.float32,
    )
    grad_values = jnp.einsum(
        "myt,myf->mtf",
        probabilities_narrow,
        gradient_attention_narrow,
        preferred_element_type=jnp.float32,
    ).reshape(row_count, value_width)
    grad_scores_low = (
        attention_probabilities
        * (grad_probs - jnp.sum(grad_probs * attention_probabilities, axis=-1, keepdims=True))
    ).astype(jnp.bfloat16)
    grad_queries = jnp.einsum(
        "sqk,skz->sqz", grad_scores_low, key_matrix, preferred_element_type=jnp.float32
    ).reshape(row_count, latent_width)
    grad_keys = jnp.einsum(
        "sqk,sqz->skz", grad_scores_low, query_rows, preferred_element_type=jnp.float32
    ).reshape(row_count, latent_width)
    grad_latent = grad_queries * score_scale * qk_affine[:, 0] + grad_keys * qk_affine[:, 1]
    grad_affine = jnp.stack(
        [
            jnp.sum(grad_queries * latent, axis=0) * score_scale,
            jnp.sum(grad_keys * latent, axis=0),
            jnp.sum(grad_queries, axis=0) * score_scale,
        ],
        axis=1,
    )
    grad_shared = jnp.concatenate([grad_latent, grad_gate], axis=1) * silu_slope(shared_pre)
    grad_update_low = (grad_update * update * (1.0 - update)).astype(jnp.bfloat16)
    grad_shared_low = grad_shared.astype(jnp.bfloat16)
    grad_proj_low = jnp.concatenate([grad_update_low, grad_shared_low, grad_add_low], axis=1)
    grad_mix_w = reduce_big(
        mixed_low,
        jnp.concatenate(
            [grad_update_low, grad_shared_low[:, latent_width:], grad_add_low], axis=1
        ),
    )
    grad_mix_latent = contract_rows(mixed_low, grad_shared_low[:, :latent_width])
    affine_rows, norm2_rows, latent_rows = reduced_small(
        [
            grad_affine.reshape(wide, -1),
            grad_norm2.reshape(wide, -1),
            grad_mix_latent.reshape(wide, -1),
        ]
    )
    grad_mixed_pre = times_transpose(grad_proj_low, w_mix) * silu_slope(mixed_pre)
    grad_omega = jnp.sum(grad_mixed_pre * normed, axis=0)
    grad_value_low = (grad_values * silu_slope(value_pre)).astype(jnp.bfloat16)
    grad_value_w = reduce_big(normed_low, grad_value_low)
    grad_tiles = grad_mixed_pre.reshape((seg_count, step_count) + tile)
    leads = scan_ends(grad_tiles, first_run, decay, True)
    later = entering(leads, whole_keep, block_decay, "wide", True)
    grad_ema_in = scan_sum(grad_tiles, keep, decay, weight, later, True)
    ema_g, ema_m = scan_grads(normed_tiles, grad_tiles, keep_next, decay, entry, later)
    grad_normed = (
        grad_mixed_pre * ema_omega
        + times_transpose(grad_value_low, w_value)
        + grad_ema_in.reshape(row_count, model_width)
    )
    grad_in_norm, grad_norm1 = norm_back(grad_normed, standard_one, inverse_one, norm1_gain)
    tokens_grad = (grad_residual + grad_in_norm).reshape(seg_count, step_count, model_width)

    def by_owner(sums):
        return jnp.moveaxis(sums.reshape(dims, wide, -1), 0, 1).reshape(wide, -1)

    norm1_rows, omega_rows, g_rows, m_rows = reduced_small(
        [
            grad_norm1.reshape(wide, -1),
            grad_omega.reshape(wide, -1),
            by_owner(ema_g),
            by_owner(ema_m),
        ]
    )
    owned = model_width // wide
    start = lax.axis_index("wide") * owned
    own_retain, own_damping, own_beta, own_eta = (
        lax.dynamic_slice_in_dim(a, start, owned, 0) for a in (retain, damping, ema_beta, ema_eta)
    )
    g_own = g_rows.reshape(dims, owned).T * (1.0 / math.sqrt(dims))
    m_own = m_rows.reshape(dims, owned).T * (1.0 / math.sqrt(dims))
    decay_grad = own_eta * own_retain * own_beta * m_own
    grad_delta = (
        (own_beta * own_eta * g_own - own_damping * decay_grad)
        * own_retain
        * (1.0 - own_retain)
    )
    grad_alpha = -own_retain * decay_grad * own_damping * (1.0 - own_damping)
    grad_beta = own_retain * own_eta * g_own
    grad_eta = own_retain * own_beta * g_own
    latent_columns = latent_rows.reshape(-1, latent_width)
    mix_width = model_width
    mix_all = jnp.concatenate(grad_mix_w, axis=1)
    mix_columns = jnp.concatenate(
        [mix_all[:, :mix_width], latent_columns, mix_all[:, mix_width:]], axis=1
    )
    return (
        result,
        tokens_grad,
        norm1_rows,
        grad_delta,
        grad_alpha,
        grad_beta,
        grad_eta,
        omega_rows,
        jnp.concatenate(grad_value_w, axis=1),
        mix_columns,
        affine_rows.reshape(-1, 3),
        jnp.concatenate(grad_hidden_w, axis=1),
        norm2_rows,
        jnp.concatenate(grad_ffn_in_w, axis=1),
        jnp.concatenate(grad_ffn_out_w, axis=1),
    )


def solution(mesh):
    in_specs = (
        P("narrow", "wide", None),
        P("narrow", "wide"),
        P(),
        P(),
        P(),
        P(),
        P(),
        P(),
        P(),
        P(),
        P(),
        P(),
        P(),
        P(),
        P(),
        P("narrow", "wide", None),
    )
    out_specs = (
        P("narrow", "wide", None),
        P("narrow", "wide", None),
        P("wide"),
        P("wide", None),
        P("wide", None),
        P("wide", None),
        P("wide", None),
        P("wide"),
        P("wide", None),
        P("wide", None),
        P("wide", None),
        P("wide", None),
        P("wide"),
        P("wide", None),
        P("wide", None),
    )
    return jax.shard_map(
        per_device, mesh=mesh, in_specs=in_specs, out_specs=out_specs, check_vma=False
    )
```
